32 devices in a mesh: beam: 8 (over y, x, core), freq: 4 (over z).
Axes of the slice: x: 2, y: 2, z: 4, core: 2. Of those that a mesh axis runs over, the one named last changes fastest.
Arguments:
- intensity: bfloat16 [8, 16384, 256], P(None, ('freq', 'beam')), may hold values from -600 to 600, as said below
- channel_mask: int32 [16384], P('freq'), may hold values 0 or 1
- box_widths: int32 [9], replicated, may hold values from 1 to 64
Outputs:
- snr_peak: float32 [8, 4096], P('beam', 'freq')
The draws below stay inside these ranges and needn't reach their ends.
Inputs may be any that keep to these rules, and one draw needn't show every extreme that they name: `intensity`: filterbank intensities of every beam and channel, of any sign.
All inputs are finite; a program needn't handle non-finite values. No bound on the sum of `channel_mask` on one device may be relied on, other than what follows from the above.
Results may differ from the reference program's by a relative error of at most 0.002.
Values may be sent and summed in bfloat16 or wider, within the bound.
A program may use at most 64 MiB of HBM per device.

```python
import jax
import jax.numpy as jnp
from jax import lax

CHANS = 16384
NDM = 4096
SAMP = 256
NWIDTH = 9
BEAMS = 8


def draw_intensity(key, part):
    key_gain, key_offset, key_noise = jax.random.split(key, 3)
    beam_pos = jnp.arange(BEAMS, dtype=jnp.float32) / max(BEAMS - 1, 1)
    beam_ramp = 3.0 ** beam_pos
    gain_field = beam_ramp[:, None] * jnp.exp(jax.random.uniform(key_gain, (BEAMS, CHANS), jnp.float32, 0.0, 2.302585))
    offsets = jax.random.uniform(key_offset, (BEAMS, CHANS), jnp.float32, -3.0, 3.0) * gain_field
    noise_field = jax.random.normal(key_noise, (BEAMS, CHANS, SAMP), jnp.float32)
    return (offsets[:, :, None] + gain_field[:, :, None] * noise_field).astype(jnp.bfloat16)


def touch_ends(entries, stream_key, low, top_value):
    spot = [jax.random.randint(jax.random.fold_in(stream_key, axis), (), 0, length) for axis, length in enumerate(entries.shape)]
    widest = entries.shape.index(max(entries.shape))
    next_to = spot[:widest] + [(spot[widest] + 1) % entries.shape[widest]] + spot[widest + 1:]
    return entries.at[tuple(spot)].set(low).at[tuple(next_to)].set(top_value)


def setup_inputs(seed: int = 0) -> dict:
    keys = jax.random.split(jax.random.key(seed), 4)
    intensity = draw_intensity(jax.random.fold_in(keys[3], 71), 0)
    channel_mask = touch_ends((jax.random.randint(keys[1], (CHANS,), 0, 8) < 7).astype(jnp.int32), jax.random.fold_in(keys[1], 1), 0, 1)
    box_widths = touch_ends(jax.random.randint(keys[2], (NWIDTH,), 1, 65), jax.random.fold_in(keys[2], 1), 1, 64).astype(jnp.int32)
    return dict(intensity=intensity, channel_mask=channel_mask, box_widths=box_widths)


epsilon = 1e-05

def statistics(channel_sum, squares, channel_mask, row_total):
    channel_mean = channel_sum / row_total
    channel_var = squares / row_total - channel_mean * channel_mean
    channel_scale = lax.rsqrt(channel_var + epsilon) * channel_mask.astype(jnp.float32)
    return (channel_scale, channel_mean)

def advance_ref(row_block, shift_rows):
    samples = row_block.shape[-1]
    padded = jnp.concatenate([row_block, jnp.zeros_like(row_block)], axis=-1)
    time_index = jnp.arange(samples, dtype=jnp.int32)
    gather_index = jnp.minimum(time_index[None, :] + shift_rows[:, None], 2 * samples - 1)
    gather_index = jnp.broadcast_to(gather_index, row_block.shape)
    return jnp.take_along_axis(padded, gather_index, axis=-1)

def dedisperse(band_rows):
    tree_rows = band_rows[:, None, :]
    band_width = 1
    trial_count = 1
    while band_width < CHANS:
        band_width = band_width * 2
        grown = max(1, band_width * NDM // CHANS)
        low_part = tree_rows[0::2]
        high_part = tree_rows[1::2]
        if grown == trial_count:
            tree_rows = low_part + high_part
        else:
            shift_rows = jnp.arange(trial_count, dtype=jnp.int32)
            even_rows = low_part + advance_ref(high_part, shift_rows)
            odd_rows = low_part + advance_ref(high_part, shift_rows + 1)
            tree_rows = jnp.stack([even_rows, odd_rows], axis=2).reshape(low_part.shape[0], 2 * trial_count, SAMP)
        trial_count = grown
    return tree_rows[0]

def boxcar_peaks(series, box_widths):
    samples = series.shape[-1]
    lead_dims = series.shape[:-1]
    prefix = jnp.concatenate([jnp.zeros(lead_dims + (1,), series.dtype), jnp.cumsum(series, axis=-1), jnp.zeros(lead_dims + (samples,), series.dtype)], axis=-1)
    time_index = jnp.arange(samples, dtype=jnp.int32)
    best_peak = None
    for number in range(box_widths.shape[0]):
        box_span = box_widths[number]
        ahead_sum = lax.dynamic_slice_in_dim(prefix, box_span, samples, axis=series.ndim - 1)
        norm_factor = lax.rsqrt((box_span * CHANS).astype(jnp.float32))
        box_sum = (ahead_sum - prefix[..., :samples]) * norm_factor
        box_sum = jnp.where(time_index <= samples - box_span, box_sum, -jnp.inf)
        width_peak = lax.optimization_barrier(jnp.max(box_sum, axis=-1))
        best_peak = width_peak if best_peak is None else jnp.maximum(best_peak, width_peak)
    return best_peak

def reference(intensity, channel_mask, box_widths):
    row_total = float(BEAMS * SAMP)
    channel_sum = lax.optimization_barrier(jnp.sum(intensity.astype(jnp.float32), axis=(0, 2)))
    squares = lax.optimization_barrier(jnp.sum(jnp.square(intensity.astype(jnp.float32)), axis=(0, 2)))
    channel_scale, channel_mean = statistics(channel_sum, squares, channel_mask, row_total)

    def one_beam(beam_rows):
        normed = ((beam_rows.astype(jnp.float32) - channel_mean[:, None]) * channel_scale[:, None]).astype(jnp.bfloat16)
        series = dedisperse(normed.astype(jnp.float32))
        return boxcar_peaks(series, box_widths)
    return lax.map(one_beam, intensity)
```

```python
import functools

import jax
import jax.numpy as jnp
from jax import lax
from jax.experimental import pallas as pl
from jax.experimental.pallas import tpu as pltpu
from jax.sharding import PartitionSpec as P

CHANS = 16384
NDM = 4096
LANE_ROWS = 8

epsilon = 1e-05


def reverse_bits(number, count):
    result = 0
    for _ in range(count):
        result = result << 1 | number & 1
        number >>= 1
    return result


def rolled(block, amount):
    samples = block.shape[-1]
    if isinstance(amount, int):
        amount = amount % samples
        return block if amount == 0 else pltpu.roll(block, samples - amount, block.ndim - 1)
    return pltpu.roll(block, (samples - 1) & (samples - amount), block.ndim - 1)


def lane_index(shape):
    return lax.broadcasted_iota(jnp.int32, shape, len(shape) - 1)


def earlier(block, amount):
    samples = block.shape[-1]
    if isinstance(amount, int) and amount == 0:
        return block
    return jnp.where(lane_index(block.shape) < samples - amount, rolled(block, amount), 0.0)


def entry_kernel(row_total, place_ref, x_ref, mask_ref, out_ref):
    rows, beams, bands, samples = out_ref.shape
    width = x_ref.shape[1]
    group = width // (bands * rows)
    total = jnp.zeros((width, samples), jnp.float32)
    squares = jnp.zeros((width, samples), jnp.float32)
    for beam in range(beams):
        wide = x_ref[beam].astype(jnp.float32)
        total = total + wide
        squares = squares + wide * wide
    channel_mean = jnp.sum(total, axis=1, keepdims=True) / row_total
    channel_var = jnp.sum(squares, axis=1, keepdims=True) / row_total - channel_mean * channel_mean
    channel_scale = lax.rsqrt(channel_var + epsilon)
    out_row = lax.broadcasted_iota(jnp.int32, (rows * bands, width), 0)
    channel = lax.broadcasted_iota(jnp.int32, (rows * bands, width), 1)
    wanted = (out_row % bands) * rows + out_row // bands
    clean = mask_ref[pl.ds(place_ref[0], 1), :].astype(jnp.float32)
    chosen = jnp.where(channel // group == wanted, clean, 0.0).astype(jnp.bfloat16)
    for beam in range(beams):
        wide = x_ref[beam].astype(jnp.float32)
        normed = ((wide - channel_mean) * channel_scale).astype(jnp.bfloat16)
        sums = jnp.dot(chosen, normed, preferred_element_type=jnp.float32)
        tree = [[sums[i * bands:(i + 1) * bands]] for i in range(rows)]
        while len(tree) > 1:
            merged = []
            for low, high in zip(tree[0::2], tree[1::2]):
                merged.append(
                    [low[m // 2] + earlier(high[m // 2], (m + 1) // 2) for m in range(2 * len(low))]
                )
            tree = merged
        for number, row in enumerate(tree[0]):
            out_ref[number, beam] = row.astype(jnp.bfloat16)


def entry_rows(intensity, mask_rows, place, rows):
    beams, width, samples = intensity.shape
    bands = width * NDM // (CHANS * rows)
    chunks = 2 if bands % 32 == 0 else 1
    return pl.pallas_call(
        functools.partial(entry_kernel, float(beams * samples)),
        grid_spec=pltpu.PrefetchScalarGridSpec(
            num_scalar_prefetch=1,
            grid=(chunks,),
            in_specs=[
                pl.BlockSpec((beams, width // chunks, samples), lambda c, p: (0, c, 0)),
                pl.BlockSpec((mask_rows.shape[0], width // chunks), lambda c, p: (0, c)),
            ],
            out_specs=pl.BlockSpec((rows, beams, bands // chunks, samples), lambda c, p: (0, 0, c, 0)),
        ),
        out_shape=jax.ShapeDtypeStruct((rows, beams, bands, samples), jnp.bfloat16),
    )(place, intensity, mask_rows)


def trial_kernel(place_ref, widths_ref, x_ref, out_ref, first, even, odd, series, boxes):
    total, samples = x_ref.shape[1:]
    tiles = total // LANE_ROWS
    tile_bits = tiles.bit_length() - 1
    block = place_ref[0]
    for high in range(LANE_ROWS):
        spot = reverse_bits(high, LANE_ROWS.bit_length() - 1)
        for part in range(samples // 128):
            first[part, spot * tiles:(spot + 1) * tiles] = x_ref[
                0, high * tiles:(high + 1) * tiles, part * 128:(part + 1) * 128
            ].astype(jnp.float32)
    for tile in range(tiles):
        for part in range(samples // 128):
            even[reverse_bits(tile, tile_bits), :, part * 128:(part + 1) * 128] = first[
                part, pl.ds(tile, LANE_ROWS, stride=tiles)
            ]

    source, target = even, odd
    count = 1
    while count < tiles:
        half = tiles // count // 2

        def merge(j, source=source, target=target, count=count, half=half):
            low = source[pl.ds(j * 2 * half, half)].reshape(half * LANE_ROWS, samples)
            high = source[pl.ds(j * 2 * half + half, half)].reshape(half * LANE_ROWS, samples)
            moved = earlier(high, block * count + j)
            target[pl.ds(2 * j * half, half)] = (low + moved).reshape(half, LANE_ROWS, samples)
            target[pl.ds((2 * j + 1) * half, half)] = (low + earlier(moved, 1)).reshape(half, LANE_ROWS, samples)

        if count <= 8:
            for j in range(count):
                merge(j)
        else:
            def step(i, carry, merge=merge):
                for k in range(8):
                    merge(i * 8 + k)
                return carry
            lax.fori_loop(0, count // 8, step, 0)
        source, target = target, source
        count = count * 2

    shape = (LANE_ROWS, samples)
    lane = lane_index(shape)
    spot = lax.broadcasted_iota(jnp.int32, shape, 0)
    bit_high, bit_mid, bit_low = spot >> 2 & 1, spot >> 1 & 1, spot & 1

    def final_rows(j):
        tree = source[j]
        row = block * tiles + j
        other = pltpu.roll(tree, 4, 0)
        low = jnp.where(bit_high == 0, tree, other)
        high = rolled(jnp.where(bit_high == 0, other, tree), row)
        high = jnp.where(bit_high == 1, rolled(high, 1), high)
        tree = low + jnp.where(lane + (row + bit_high) < samples, high, 0.0)
        low = jnp.where(bit_mid == 0, tree, pltpu.roll(tree, 2, 0))
        high = rolled(jnp.where(bit_mid == 0, pltpu.roll(tree, LANE_ROWS - 2, 0), tree), 2 * row)
        high = jnp.where(bit_high == 1, rolled(high, 1), high)
        high = jnp.where(bit_mid == 1, rolled(high, 1), high)
        tree = low + jnp.where(lane + (2 * row + bit_high + bit_mid) < samples, high, 0.0)
        low = jnp.where(bit_low == 0, tree, pltpu.roll(tree, 1, 0))
        high = rolled(jnp.where(bit_low == 0, pltpu.roll(tree, LANE_ROWS - 1, 0), tree), 4 * row)
        high = jnp.where(bit_high == 1, rolled(high, 2), high)
        high = jnp.where(bit_mid == 1, rolled(high, 1), high)
        high = jnp.where(bit_low == 1, rolled(high, 1), high)
        return low + jnp.where(lane + (4 * row + 2 * bit_high + bit_mid + bit_low) < samples, high, 0.0)

    def finish(i, carry):
        for k in range(4):
            pair = i * 4 + k
            rows = jnp.concatenate([final_rows(2 * pair), final_rows(2 * pair + 1)], axis=0)
            coarse = rows.astype(jnp.bfloat16)
            place = pl.ds(pl.multiple_of(pair * 16, 16), 16)
            series[place, :samples] = coarse
            series[place, samples:] = (rows - coarse.astype(jnp.float32)).astype(jnp.bfloat16)
        return carry

    lax.fori_loop(0, tiles // 8, finish, 0)

    start = lax.broadcasted_iota(jnp.int32, (samples, samples), 0)
    time = lax.broadcasted_iota(jnp.int32, (samples, samples), 1)
    piece = 256
    for number in range(widths_ref.shape[0]):
        width = widths_ref[number]
        begin = jnp.minimum(start, samples - width)
        inside = jnp.where((time >= begin) & (time < begin + width), 1.0, 0.0).astype(jnp.bfloat16)
        boxes[number, :, :samples] = inside
        boxes[number, :, samples:] = inside
    for part in range(total // piece):
        rows = series[part * piece:(part + 1) * piece]
        best = None
        for number in range(widths_ref.shape[0]):
            sums = lax.dot_general(
                boxes[number], rows, (((1,), (1,)), ((), ())), preferred_element_type=jnp.float32
            )
            norm = lax.rsqrt(jnp.full((1, piece), widths_ref[number] * CHANS, jnp.int32).astype(jnp.float32))
            peak = jnp.max(sums, axis=0, keepdims=True) * norm
            best = peak if best is None else jnp.maximum(best, peak)
        out_ref[0, :, part * piece:(part + 1) * piece] = best


def trial_peaks(rows, box_widths, place):
    beams, total, samples = rows.shape
    tiles = total // LANE_ROWS
    widths = box_widths.shape[0]
    return pl.pallas_call(
        trial_kernel,
        grid_spec=pltpu.PrefetchScalarGridSpec(
            num_scalar_prefetch=2,
            grid=(beams,),
            in_specs=[pl.BlockSpec((1, total, samples), lambda b, p, w: (b, 0, 0))],
            out_specs=pl.BlockSpec((1, 1, total), lambda b, p, w: (b, 0, 0)),
            scratch_shapes=[
                pltpu.VMEM((samples // 128, total, 128), jnp.float32),
                pltpu.VMEM((tiles, LANE_ROWS, samples), jnp.float32),
                pltpu.VMEM((tiles, LANE_ROWS, samples), jnp.float32),
                pltpu.VMEM((total, 2 * samples), jnp.bfloat16),
                pltpu.VMEM((widths, samples, 2 * samples), jnp.bfloat16),
            ],
        ),
        out_shape=jax.ShapeDtypeStruct((beams, 1, total), jnp.float32),
    )(place, box_widths, rows)[:, 0]


def shards(intensity, channel_mask, box_widths):
    group_count = lax.axis_size("beam")
    band_count = lax.axis_size("freq")
    beams_all, piece_width, samples = intensity.shape
    beam_dev = beams_all // group_count
    beam_place = lax.axis_index("beam").reshape(1)
    freq_place = lax.axis_index("freq").reshape(1)
    mask_rows = channel_mask.reshape(group_count, piece_width)
    rows = entry_rows(intensity, mask_rows, beam_place, band_count)
    bands = rows.shape[2]
    rows = rows.reshape(band_count * group_count, beam_dev * bands, samples)
    rows = lax.all_to_all(rows, ("freq", "beam"), split_axis=0, concat_axis=0, tiled=True)
    rows = rows.reshape(band_count * group_count, beam_dev, bands, samples)
    rows = jnp.swapaxes(rows, 0, 1).reshape(beam_dev, -1, samples)
    return trial_peaks(rows, box_widths, freq_place)


def solution(mesh):
    in_specs = (P(None, ("freq", "beam"), None), P("freq"), P())
    out_specs = P("beam", "freq")
    return jax.shard_map(shards, mesh=mesh, in_specs=in_specs, out_specs=out_specs, check_vma=False)
```

```python
import functools

import jax
import jax.numpy as jnp
from jax import lax
from jax.experimental import pallas as pl
from jax.experimental.pallas import tpu as pltpu
from jax.sharding import PartitionSpec as P

CHANS = 16384
NDM = 4096
LANE_ROWS = 8
LANES = 128
WIDEST = 64

epsilon = 1e-05


def reverse_bits(number, count):
    result = 0
    for _ in range(count):
        result = result << 1 | number & 1
        number >>= 1
    return result


def lane_index(shape):
    return lax.broadcasted_iota(jnp.int32, shape, len(shape) - 1)


def earlier(block, amount):
    if amount == 0:
        return block
    samples = block.shape[-1]
    return jnp.where(lane_index(block.shape) < samples - amount, pltpu.roll(block, samples - amount, 1), 0.0)


def entry_kernel(row_total, place_ref, x_ref, mask_ref, out_ref):
    rows, beams, bands, samples = out_ref.shape
    width = x_ref.shape[1]
    group = width // (bands * rows)
    total = jnp.zeros((width, samples), jnp.float32)
    squares = jnp.zeros((width, samples), jnp.float32)
    for beam in range(beams):
        wide = x_ref[beam].astype(jnp.float32)
        total = total + wide
        squares = squares + wide * wide
    channel_mean = jnp.sum(total, axis=1, keepdims=True) / row_total
    channel_var = jnp.sum(squares, axis=1, keepdims=True) / row_total - channel_mean * channel_mean
    channel_scale = lax.rsqrt(channel_var + epsilon)
    out_row = lax.broadcasted_iota(jnp.int32, (rows * bands, width), 0)
    channel = lax.broadcasted_iota(jnp.int32, (rows * bands, width), 1)
    wanted = (out_row % bands) * rows + out_row // bands
    clean = mask_ref[pl.ds(place_ref[0], 1), :].astype(jnp.float32)
    chosen = jnp.where(channel // group == wanted, clean, 0.0).astype(jnp.bfloat16)
    for beam in range(beams):
        wide = x_ref[beam].astype(jnp.float32)
        normed = ((wide - channel_mean) * channel_scale).astype(jnp.bfloat16)
        sums = jnp.dot(chosen, normed, preferred_element_type=jnp.float32)
        tree = [[sums[i * bands:(i + 1) * bands]] for i in range(rows)]
        while len(tree) > 1:
            merged = []
            for low, high in zip(tree[0::2], tree[1::2]):
                merged.append(
                    [low[m // 2] + earlier(high[m // 2], (m + 1) // 2) for m in range(2 * len(low))]
                )
            tree = merged
        for number, row in enumerate(tree[0]):
            out_ref[number, beam] = row.astype(jnp.bfloat16)


def entry_rows(intensity, mask_rows, place, rows):
    beams, width, samples = intensity.shape
    bands = width * NDM // (CHANS * rows)
    chunks = 2 if bands % 32 == 0 else 1
    return pl.pallas_call(
        functools.partial(entry_kernel, float(beams * samples)),
        grid_spec=pltpu.PrefetchScalarGridSpec(
            num_scalar_prefetch=1,
            grid=(chunks,),
            in_specs=[
                pl.BlockSpec((beams, width // chunks, samples), lambda c, p: (0, c, 0)),
                pl.BlockSpec((mask_rows.shape[0], width // chunks), lambda c, p: (0, c)),
            ],
            out_specs=pl.BlockSpec((rows, beams, bands // chunks, samples), lambda c, p: (0, 0, c, 0)),
        ),
        out_shape=jax.ShapeDtypeStruct((rows, beams, bands, samples), jnp.bfloat16),
    )(place, intensity, mask_rows)


def advanced(pieces, amount):
    lanes = pieces[0].shape[-1]
    position = lane_index(pieces[0].shape)
    turn = (lanes - amount) & (lanes - 1)
    turned = [pltpu.roll(piece, turn, 1) for piece in pieces]
    return joined(turned, lambda limit: position < limit - amount)


def advanced_rows(pieces, amounts):
    lanes = pieces[0].shape[-1]
    position = lane_index(pieces[0].shape) + amounts
    picks = position & (lanes - 1)
    turned = [jnp.take_along_axis(piece, picks, axis=1, mode="promise_in_bounds") for piece in pieces]
    return joined(turned, lambda limit: position < limit)


def joined(turned, below):
    lanes = turned[0].shape[-1]
    near = [below((k + 1) * lanes) for k in range(len(turned))]
    result = []
    for number in range(len(turned)):
        value = jnp.zeros_like(turned[0])
        for ahead in reversed(range(len(turned) - number)):
            value = jnp.where(near[ahead], turned[number + ahead], value)
        result.append(value)
    return result


def trial_kernel(place_ref, widths_ref, x_ref, out_ref, first, even, odd, series, prefix):
    total, samples = x_ref.shape[1:]
    tiles = total // LANE_ROWS
    tile_bits = tiles.bit_length() - 1
    lanes = prefix.shape[2]
    parts = samples // lanes
    pitch = first.shape[1] // LANE_ROWS
    block = place_ref[0]
    for high in range(LANE_ROWS):
        spot = reverse_bits(high, LANE_ROWS.bit_length() - 1)
        for part in range(parts):
            first[part, spot * pitch:spot * pitch + tiles] = x_ref[
                0, high * tiles:(high + 1) * tiles, part * lanes:(part + 1) * lanes
            ].astype(jnp.float32)
    for tile in range(tiles):
        for part in range(parts):
            even[reverse_bits(tile, tile_bits), :, part * lanes:(part + 1) * lanes] = first[
                part, pl.ds(tile, LANE_ROWS, stride=pitch)
            ]

    source, target = even, odd
    count = 1
    while count < tiles:
        half = tiles // count // 2

        def merge(j, source=source, target=target, count=count, half=half):
            flat = (half * LANE_ROWS, lanes)
            cut = [slice(part * lanes, (part + 1) * lanes) for part in range(parts)]
            low = [source[pl.ds(j * 2 * half, half), :, c].reshape(flat) for c in cut]
            high = [source[pl.ds(j * 2 * half + half, half), :, c].reshape(flat) for c in cut]
            for side in range(2):
                moved = advanced(high, block * count + j + side)
                for c, base, extra in zip(cut, low, moved):
                    target[pl.ds((2 * j + side) * half, half), :, c] = (base + extra).reshape(
                        half, LANE_ROWS, lanes
                    )

        if count <= 16:
            for j in range(count):
                merge(j)
        else:
            def step(i, carry, merge=merge):
                for k in range(32):
                    merge(i * 32 + k)
                return carry
            lax.fori_loop(0, count // 32, step, 0)
        source, target = target, source
        count = count * 2

    spot = lax.broadcasted_iota(jnp.int32, (LANE_ROWS, lanes), 0)
    bits = [spot >> 2 & 1, spot >> 1 & 1, spot & 1]
    clear = [bit == 0 for bit in bits]

    def final_rows(j):
        pieces = [source[j, :, part * lanes:(part + 1) * lanes] for part in range(parts)]
        row = spot * 0 + (block * tiles + j)
        for level, reach in enumerate((4, 2, 1)):
            low, high = [], []
            for piece in pieces:
                down = pltpu.roll(piece, reach, 0)
                up = down if 2 * reach == LANE_ROWS else pltpu.roll(piece, LANE_ROWS - reach, 0)
                low.append(jnp.where(clear[level], piece, down))
                high.append(jnp.where(clear[level], up, piece))
            moved = advanced_rows(high, row + bits[level])
            pieces = [base + extra for base, extra in zip(low, moved)]
            row = 2 * row + bits[level]
        return jnp.concatenate(pieces, axis=1)

    def finish(i, carry):
        for k in range(16):
            pair = i * 16 + k
            rows = jnp.concatenate([final_rows(2 * pair), final_rows(2 * pair + 1)], axis=0)
            coarse = rows.astype(jnp.bfloat16)
            place = pl.ds(pl.multiple_of(pair * 16, 16), 16)
            series[place, :samples] = coarse
            series[place, samples:] = (rows - coarse.astype(jnp.float32)).astype(jnp.bfloat16)
        return carry

    lax.fori_loop(0, tiles // 32, finish, 0)

    until = lax.broadcasted_iota(jnp.int32, (samples, 2 * samples), 0)
    time = lax.broadcasted_iota(jnp.int32, (samples, 2 * samples), 1) & (samples - 1)
    ladder = jnp.where(time <= until, 1.0, 0.0).astype(jnp.bfloat16)
    margin = prefix.shape[1] - samples - LANE_ROWS
    piece = 2 * lanes
    for part in range(total // piece):
        sums = lax.dot_general(
            ladder, series[part * piece:(part + 1) * piece], (((1,), (1,)), ((), ())),
            preferred_element_type=jnp.float32,
        )
        for side in range(2):
            column = 2 * part + side
            prefix[column, :LANE_ROWS] = jnp.zeros((LANE_ROWS, lanes), jnp.float32)
            prefix[column, LANE_ROWS:LANE_ROWS + samples] = sums[:, side * lanes:(side + 1) * lanes]
            prefix[column, LANE_ROWS + samples:] = jnp.full((margin, lanes), -jnp.inf, jnp.float32)
    for column in range(total // lanes):
        best = None
        for number in range(widths_ref.shape[0]):
            width = widths_ref[number]
            sums = (
                prefix[column, pl.ds(LANE_ROWS - 1 + width, samples)]
                - prefix[column, LANE_ROWS - 1:LANE_ROWS - 1 + samples]
            )
            norm = lax.rsqrt(jnp.full((1, lanes), width * CHANS, jnp.int32).astype(jnp.float32))
            peak = jnp.max(sums, axis=0, keepdims=True) * norm
            best = peak if best is None else jnp.maximum(best, peak)
        out_ref[0, :, column * lanes:(column + 1) * lanes] = best


def trial_peaks(rows, box_widths, place):
    beams, total, samples = rows.shape
    tiles = total // LANE_ROWS
    return pl.pallas_call(
        trial_kernel,
        grid_spec=pltpu.PrefetchScalarGridSpec(
            num_scalar_prefetch=2,
            grid=(beams,),
            in_specs=[pl.BlockSpec((1, total, samples), lambda b, p, w: (b, 0, 0))],
            out_specs=pl.BlockSpec((1, 1, total), lambda b, p, w: (b, 0, 0)),
            scratch_shapes=[
                pltpu.VMEM((samples // LANES, total + LANE_ROWS * LANE_ROWS, LANES), jnp.float32),
                pltpu.VMEM((tiles, LANE_ROWS, samples), jnp.float32),
                pltpu.VMEM((tiles, LANE_ROWS, samples), jnp.float32),
                pltpu.VMEM((total, 2 * samples), jnp.bfloat16),
                pltpu.VMEM((total // LANES, LANE_ROWS + samples + WIDEST, LANES), jnp.float32),
            ],
        ),
        out_shape=jax.ShapeDtypeStruct((beams, 1, total), jnp.float32),
    )(place, box_widths, rows)[:, 0]


def shards(intensity, channel_mask, box_widths):
    group_count = lax.axis_size("beam")
    band_count = lax.axis_size("freq")
    beams_all, piece_width, samples = intensity.shape
    beam_dev = beams_all // group_count
    beam_place = lax.axis_index("beam").reshape(1)
    freq_place = lax.axis_index("freq").reshape(1)
    mask_rows = channel_mask.reshape(group_count, piece_width)
    rows = entry_rows(intensity, mask_rows, beam_place, band_count)
    bands = rows.shape[2]
    rows = rows.reshape(band_count * group_count, beam_dev * bands, samples)
    rows = lax.all_to_all(rows, ("freq", "beam"), split_axis=0, concat_axis=0, tiled=True)
    rows = rows.reshape(band_count * group_count, beam_dev, bands, samples)
    rows = jnp.swapaxes(rows, 0, 1).reshape(beam_dev, -1, samples)
    return trial_peaks(rows, box_widths, freq_place)


def solution(mesh):
    in_specs = (P(None, ("freq", "beam"), None), P("freq"), P())
    out_specs = P("beam", "freq")
    return jax.shard_map(shards, mesh=mesh, in_specs=in_specs, out_specs=out_specs, check_vma=False)
```

```python
import jax
import jax.numpy as jnp
from jax import lax
from jax.experimental import pallas as pl
from jax.experimental.pallas import tpu as pltpu
from jax.sharding import PartitionSpec as P

CHANS = 16384
NDM = 4096
LANE_ROWS = 8
LANES = 128
WIDEST = 64

epsilon = 1e-05


def reverse_bits(number, count):
    result = 0
    for _ in range(count):
        result = result << 1 | number & 1
        number >>= 1
    return result


def lane_index(shape):
    return lax.broadcasted_iota(jnp.int32, shape, len(shape) - 1)


def earlier(block, amount):
    if amount == 0:
        return block
    samples = block.shape[-1]
    return jnp.where(lane_index(block.shape) < samples - amount, pltpu.roll(block, samples - amount, 1), 0.0)


def folds(trial_dev, samples):
    return trial_dev >= 4 * samples


def channel_limits(trial_dev, blocks, samples):
    limits = []
    for block in range(blocks):
        limit, rows = CHANS, NDM
        while (block * trial_dev * rows // NDM + 1) // 2 >= samples:
            limit, rows = limit // 2, rows // 2
        limits.append(limit)
    return limits


def entry_kernel(x_ref, mask_ref, out_ref, send, send_sem, recv_sem, own_sem):
    blocks, beams, bands, samples = send.shape
    groups = lax.axis_size("beam")
    beam_dev = beams // groups
    width = x_ref.shape[1]
    group = width // (bands * blocks)
    trial_dev = NDM // blocks
    row_total = float(beams * samples)
    fold = folds(trial_dev, samples)
    limits = channel_limits(trial_dev, blocks, samples)
    my_block = lax.axis_index("freq")
    my_group = lax.axis_index("beam")
    my_place = my_block * groups + my_group
    devices = blocks * groups

    barrier = pltpu.get_barrier_semaphore()
    for step in range(1, devices):
        peer = (my_place + step) % devices
        pl.semaphore_signal(
            barrier, inc=1, device_id={"freq": peer // groups, "beam": peer % groups},
            device_id_type=pl.DeviceIdType.MESH,
        )

    total = jnp.zeros((width, samples), jnp.float32)
    squares = jnp.zeros((width, samples), jnp.float32)
    for beam in range(beams):
        wide = x_ref[beam].astype(jnp.float32)
        total = total + wide
        squares = squares + wide * wide
    channel_mean = jnp.sum(total, axis=1, keepdims=True) / row_total
    channel_var = jnp.sum(squares, axis=1, keepdims=True) / row_total - channel_mean * channel_mean
    channel_scale = lax.rsqrt(channel_var + epsilon)
    out_row = lax.broadcasted_iota(jnp.int32, (blocks * bands, width), 0)
    channel = lax.broadcasted_iota(jnp.int32, (blocks * bands, width), 1)
    band = out_row % bands
    if fold:
        half = bands // 2
        band = (band % half) * 2 + band // half
    wanted = band * blocks + out_row // bands
    clean = mask_ref[:, pl.ds(pl.multiple_of(my_group * width, width), width)].astype(jnp.float32)
    chosen = jnp.where(channel // group == wanted, clean, 0.0).astype(jnp.bfloat16)
    upper = my_block * 2 >= blocks

    def message(block, slot, beam, rows):
        return pltpu.make_async_remote_copy(
            src_ref=send.at[block, slot, pl.ds(0, rows)],
            dst_ref=out_ref.at[beam % beam_dev, my_place, pl.ds(0, rows)],
            send_sem=send_sem.at[block, slot],
            recv_sem=recv_sem.at[beam % beam_dev, my_place],
            device_id={"freq": block, "beam": beam // beam_dev},
            device_id_type=pl.DeviceIdType.MESH,
        )

    def own_copy(slot, part):
        return pltpu.make_async_copy(
            send.at[my_block, slot], out_ref.at[part, my_place], own_sem.at[part]
        )

    def every_message(action, slot):
        beam = (my_group * beam_dev + slot) % beams
        for block in range(blocks):
            goes = my_place * width < limits[block]
            if slot < beam_dev:
                goes = goes & (my_block != block)
            if fold:
                @pl.when(goes & upper)
                def _(block=block):
                    action(message(block, slot, beam, bands // 2))
                goes = goes & jnp.logical_not(upper)

            @pl.when(goes)
            def _(block=block):
                action(message(block, slot, beam, bands))

    for slot in range(beams):
        beam = (my_group * beam_dev + slot) % beams
        wide = x_ref[beam].astype(jnp.float32)
        normed = ((wide - channel_mean) * channel_scale).astype(jnp.bfloat16)
        sums = jnp.dot(chosen, normed, preferred_element_type=jnp.float32)
        tree = [[sums[i * bands:(i + 1) * bands]] for i in range(blocks)]
        while len(tree) > 1:
            merged = []
            for low, high in zip(tree[0::2], tree[1::2]):
                merged.append(
                    [low[m // 2] + earlier(high[m // 2], (m + 1) // 2) for m in range(2 * len(low))]
                )
            tree = merged
        for number, row in enumerate(tree[0]):
            if fold:
                both = row[:half] + row[half:]
                row = jnp.concatenate([jnp.where(upper, both, row[:half]), row[half:]], axis=0)
            send[number, slot] = row.astype(jnp.bfloat16)
        if slot == 0:
            pl.semaphore_wait(barrier, devices - 1)
        every_message(lambda copy: copy.start(), slot)
        if slot < beam_dev:
            own_copy(slot, slot).start()

    for slot in range(beam_dev):
        own_copy(slot, slot).wait()
    limit = sum(jnp.where(my_block == block, limits[block], 0) for block in range(blocks))
    for place in range(devices):
        for part in range(beam_dev):
            rows = bands // 2 if fold and 2 * place >= devices else bands
            target = out_ref.at[part, place, pl.ds(0, rows)]
            @pl.when((place * width < limit) & (place != my_place))
            def _(target=target, place=place, part=part):
                pltpu.make_async_remote_copy(
                    src_ref=target, dst_ref=target, send_sem=send_sem.at[0, 0],
                    recv_sem=recv_sem.at[part, place],
                    device_id={"freq": my_block, "beam": my_group},
                    device_id_type=pl.DeviceIdType.MESH,
                ).wait_recv()
    for slot in range(beams):
        every_message(lambda copy: copy.wait_send(), slot)


def entry_rows(intensity, channel_mask):
    beams, width, samples = intensity.shape
    blocks, groups = lax.axis_size("freq"), lax.axis_size("beam")
    bands = width * NDM // (CHANS * blocks)
    beam_dev, devices = beams // groups, blocks * groups
    return pl.pallas_call(
        entry_kernel,
        in_specs=[pl.BlockSpec(memory_space=pltpu.VMEM)] * 2,
        out_specs=pl.BlockSpec(memory_space=pl.ANY),
        scratch_shapes=[
            pltpu.VMEM((blocks, beams, bands, samples), jnp.bfloat16),
            pltpu.SemaphoreType.DMA((blocks, beams)),
            pltpu.SemaphoreType.DMA((beam_dev, devices)),
            pltpu.SemaphoreType.DMA((beam_dev,)),
        ],
        out_shape=jax.ShapeDtypeStruct((beam_dev, devices, bands, samples), jnp.bfloat16),
        compiler_params=pltpu.CompilerParams(collective_id=0, has_side_effects=True),
    )(intensity, channel_mask.reshape(1, -1))


def advanced(pieces, amount):
    lanes = pieces[0].shape[-1]
    position = lane_index(pieces[0].shape)
    turn = (lanes - amount) & (lanes - 1)
    turned = [pltpu.roll(piece, turn, 1) for piece in pieces]
    return joined(turned, lambda limit: position < limit - amount)


def advanced_rows(pieces, amounts):
    lanes = pieces[0].shape[-1]
    position = lane_index(pieces[0].shape) + amounts
    picks = position & (lanes - 1)
    turned = [jnp.take_along_axis(piece, picks, axis=1, mode="promise_in_bounds") for piece in pieces]
    return joined(turned, lambda limit: position < limit)


def joined(turned, below):
    lanes = turned[0].shape[-1]
    near = [below((k + 1) * lanes) for k in range(len(turned))]
    result = []
    for number in range(len(turned)):
        value = jnp.zeros_like(turned[0])
        for ahead in reversed(range(len(turned) - number)):
            value = jnp.where(near[ahead], turned[number + ahead], value)
        result.append(value)
    return result


def trial_kernel(place_ref, widths_ref, x_ref, out_ref, first, even, odd, series, prefix):
    total, samples = out_ref.shape[2], x_ref.shape[3]
    tiles = total // LANE_ROWS
    tile_bits = tiles.bit_length() - 1
    lanes = prefix.shape[2]
    parts = samples // lanes
    pitch = first.shape[1] // LANE_ROWS
    block = place_ref[0]
    bands = x_ref.shape[2]
    fold = folds(total, samples)
    half_bands = bands // 2
    sources = x_ref.shape[1]
    for number in range(sources):
        high, start = divmod(number * bands, tiles)
        start += reverse_bits(high, LANE_ROWS.bit_length() - 1) * pitch
        for part in range(parts):
            cut = slice(part * lanes, (part + 1) * lanes)
            if fold and 2 * number >= sources:
                first[part, start:start + half_bands] = x_ref[0, number, :half_bands, cut].astype(jnp.float32)
                first[part, start + half_bands:start + bands] = jnp.zeros((half_bands, lanes), jnp.float32)
            else:
                first[part, start:start + bands] = x_ref[0, number, :, cut].astype(jnp.float32)
    for tile in range(tiles):
        spot = tile
        if fold:
            band = tile % bands
            spot = tile - band + (band % 2) * half_bands + band // 2
        for part in range(parts):
            even[reverse_bits(tile, tile_bits), :, part * lanes:(part + 1) * lanes] = first[
                part, pl.ds(spot, LANE_ROWS, stride=pitch)
            ]

    source, target = even, odd
    count = 1
    while count < tiles:
        half = tiles // count // 2

        def merge(j, source=source, target=target, count=count, half=half):
            flat = (half * LANE_ROWS, lanes)
            cut = [slice(part * lanes, (part + 1) * lanes) for part in range(parts)]
            low = [source[pl.ds(j * 2 * half, half), :, c].reshape(flat) for c in cut]
            high = [source[pl.ds(j * 2 * half + half, half), :, c].reshape(flat) for c in cut]
            for side in range(2):
                moved = advanced(high, block * count + j + side)
                for c, base, extra in zip(cut, low, moved):
                    target[pl.ds((2 * j + side) * half, half), :, c] = (base + extra).reshape(
                        half, LANE_ROWS, lanes
                    )

        if count <= 16:
            for j in range(count):
                merge(j)
        else:
            def step(i, carry, merge=merge):
                for k in range(32):
                    merge(i * 32 + k)
                return carry
            lax.fori_loop(0, count // 32, step, 0)
        source, target = target, source
        count = count * 2

    spot = lax.broadcasted_iota(jnp.int32, (LANE_ROWS, lanes), 0)
    bits = [spot >> 2 & 1, spot >> 1 & 1, spot & 1]
    clear = [bit == 0 for bit in bits]

    def final_rows(j):
        pieces = [source[j, :, part * lanes:(part + 1) * lanes] for part in range(parts)]
        row = spot * 0 + (block * tiles + j)
        for level, reach in enumerate((4, 2, 1)):
            low, high = [], []
            for piece in pieces:
                down = pltpu.roll(piece, reach, 0)
                up = down if 2 * reach == LANE_ROWS else pltpu.roll(piece, LANE_ROWS - reach, 0)
                low.append(jnp.where(clear[level], piece, down))
                high.append(jnp.where(clear[level], up, piece))
            moved = advanced_rows(high, row + bits[level])
            pieces = [base + extra for base, extra in zip(low, moved)]
            row = 2 * row + bits[level]
        return jnp.concatenate(pieces, axis=1)

    def finish(i, carry):
        for k in range(16):
            pair = i * 16 + k
            rows = jnp.concatenate([final_rows(2 * pair), final_rows(2 * pair + 1)], axis=0)
            coarse = rows.astype(jnp.bfloat16)
            place = pl.ds(pl.multiple_of(pair * 16, 16), 16)
            series[place, :samples] = coarse
            series[place, samples:] = (rows - coarse.astype(jnp.float32)).astype(jnp.bfloat16)
        return carry

    lax.fori_loop(0, tiles // 32, finish, 0)

    until = lax.broadcasted_iota(jnp.int32, (samples, 2 * samples), 0)
    time = lax.broadcasted_iota(jnp.int32, (samples, 2 * samples), 1) & (samples - 1)
    ladder = jnp.where(time <= until, 1.0, 0.0).astype(jnp.bfloat16)
    margin = prefix.shape[1] - samples - LANE_ROWS
    piece = 2 * lanes
    for part in range(total // piece):
        sums = lax.dot_general(
            ladder, series[part * piece:(part + 1) * piece], (((1,), (1,)), ((), ())),
            preferred_element_type=jnp.float32,
        )
        for side in range(2):
            column = 2 * part + side
            prefix[column, :LANE_ROWS] = jnp.zeros((LANE_ROWS, lanes), jnp.float32)
            prefix[column, LANE_ROWS:LANE_ROWS + samples] = sums[:, side * lanes:(side + 1) * lanes]
            prefix[column, LANE_ROWS + samples:] = jnp.full((margin, lanes), -jnp.inf, jnp.float32)
    for column in range(total // lanes):
        best = None
        for number in range(widths_ref.shape[0]):
            width = widths_ref[number]
            sums = (
                prefix[column, pl.ds(LANE_ROWS - 1 + width, samples)]
                - prefix[column, LANE_ROWS - 1:LANE_ROWS - 1 + samples]
            )
            norm = lax.rsqrt(jnp.full((1, lanes), width * CHANS, jnp.int32).astype(jnp.float32))
            peak = jnp.max(sums, axis=0, keepdims=True) * norm
            best = peak if best is None else jnp.maximum(best, peak)
        out_ref[0, :, column * lanes:(column + 1) * lanes] = best


def trial_peaks(rows, box_widths, place):
    beams, devices, bands, samples = rows.shape
    total = devices * bands
    tiles = total // LANE_ROWS
    return pl.pallas_call(
        trial_kernel,
        grid_spec=pltpu.PrefetchScalarGridSpec(
            num_scalar_prefetch=2,
            grid=(beams,),
            in_specs=[pl.BlockSpec((1, devices, bands, samples), lambda b, p, w: (b, 0, 0, 0))],
            out_specs=pl.BlockSpec((1, 1, total), lambda b, p, w: (b, 0, 0)),
            scratch_shapes=[
                pltpu.VMEM((samples // LANES, total + LANE_ROWS * LANE_ROWS, LANES), jnp.float32),
                pltpu.VMEM((tiles, LANE_ROWS, samples), jnp.float32),
                pltpu.VMEM((tiles, LANE_ROWS, samples), jnp.float32),
                pltpu.VMEM((total, 2 * samples), jnp.bfloat16),
                pltpu.VMEM((total // LANES, LANE_ROWS + samples + WIDEST, LANES), jnp.float32),
            ],
        ),
        out_shape=jax.ShapeDtypeStruct((beams, 1, total), jnp.float32),
    )(place, box_widths, rows)[:, 0]


def shards(intensity, channel_mask, box_widths):
    rows = entry_rows(intensity, channel_mask)
    return trial_peaks(rows, box_widths, lax.axis_index("freq").reshape(1))


def solution(mesh):
    in_specs = (P(None, ("freq", "beam"), None), P("freq"), P())
    out_specs = P("beam", "freq")
    return jax.shard_map(shards, mesh=mesh, in_specs=in_specs, out_specs=out_specs, check_vma=False)
```

```python
import jax
import jax.numpy as jnp
from jax import lax
from jax.experimental import pallas as pl
from jax.experimental.pallas import tpu as pltpu
from jax.sharding import PartitionSpec as P

CHANS = 16384
NDM = 4096
LANE_ROWS = 8
LANES = 128
WIDEST = 64

epsilon = 1e-05


def reverse_bits(number, count):
    result = 0
    for _ in range(count):
        result = result << 1 | number & 1
        number >>= 1
    return result


def lane_index(shape):
    return lax.broadcasted_iota(jnp.int32, shape, len(shape) - 1)


def earlier(block, amount):
    if amount == 0:
        return block
    samples = block.shape[-1]
    return jnp.where(lane_index(block.shape) < samples - amount, pltpu.roll(block, samples - amount, 1), 0.0)


def folds(trial_dev, samples):
    return trial_dev >= 4 * samples


def channel_limits(trial_dev, blocks, samples):
    limits = []
    for block in range(blocks):
        limit, rows = CHANS, NDM
        while (block * trial_dev * rows // NDM + 1) // 2 >= samples:
            limit, rows = limit // 2, rows // 2
        limits.append(limit)
    return limits


def entry_kernel(x_hbm, mask_ref, out_ref, x_ref, in_sem, send, send_sem, recv_sem, own_sem):
    blocks, beams, bands, samples = send.shape
    groups = lax.axis_size("beam")
    beam_dev = beams // groups
    width = x_ref.shape[1]
    group = width // (bands * blocks)
    trial_dev = NDM // blocks
    row_total = float(beams * samples)
    fold = folds(trial_dev, samples)
    limits = channel_limits(trial_dev, blocks, samples)
    my_block = lax.axis_index("freq")
    my_group = lax.axis_index("beam")
    my_place = my_block * groups + my_group
    devices = blocks * groups

    barrier = pltpu.get_barrier_semaphore()
    for step in range(1, devices):
        peer = (my_place + step) % devices
        pl.semaphore_signal(
            barrier, inc=1, device_id={"freq": peer // groups, "beam": peer % groups},
            device_id_type=pl.DeviceIdType.MESH,
        )

    chunks = in_sem.shape[0]
    span = width // chunks
    loads = [
        pltpu.make_async_copy(
            x_hbm.at[:, pl.ds(c * span, span)], x_ref.at[:, pl.ds(c * span, span)], in_sem.at[c]
        )
        for c in range(chunks)
    ]
    for load in loads:
        load.start()
    means, scales = [], []
    for c in range(chunks):
        loads[c].wait()
        total = jnp.zeros((span, samples), jnp.float32)
        squares = jnp.zeros((span, samples), jnp.float32)
        for beam in range(beams):
            wide = x_ref[beam, c * span:(c + 1) * span].astype(jnp.float32)
            total = total + wide
            squares = squares + wide * wide
        mean = jnp.sum(total, axis=1, keepdims=True) / row_total
        var = jnp.sum(squares, axis=1, keepdims=True) / row_total - mean * mean
        means.append(mean)
        scales.append(lax.rsqrt(var + epsilon))
    channel_mean = jnp.concatenate(means, axis=0)
    channel_scale = jnp.concatenate(scales, axis=0)
    out_row = lax.broadcasted_iota(jnp.int32, (blocks * bands, width), 0)
    channel = lax.broadcasted_iota(jnp.int32, (blocks * bands, width), 1)
    band = out_row % bands
    if fold:
        half = bands // 2
        band = (band % half) * 2 + band // half
    wanted = band * blocks + out_row // bands
    clean = mask_ref[:, pl.ds(pl.multiple_of(my_group * width, width), width)].astype(jnp.float32)
    chosen = jnp.where(channel // group == wanted, clean, 0.0).astype(jnp.bfloat16)
    upper = my_block * 2 >= blocks

    def message(block, slot, beam, rows):
        return pltpu.make_async_remote_copy(
            src_ref=send.at[block, slot, pl.ds(0, rows)],
            dst_ref=out_ref.at[beam % beam_dev, my_place, pl.ds(0, rows)],
            send_sem=send_sem.at[block, slot],
            recv_sem=recv_sem.at[beam % beam_dev, my_place],
            device_id={"freq": block, "beam": beam // beam_dev},
            device_id_type=pl.DeviceIdType.MESH,
        )

    def own_copy(slot, part):
        return pltpu.make_async_copy(
            send.at[my_block, slot], out_ref.at[part, my_place], own_sem.at[part]
        )

    def every_message(action, slot):
        beam = (my_group * beam_dev + slot) % beams
        for block in range(blocks):
            goes = my_place * width < limits[block]
            if slot < beam_dev:
                goes = goes & (my_block != block)
            if fold:
                @pl.when(goes & upper)
                def _(block=block):
                    action(message(block, slot, beam, bands // 2))
                goes = goes & jnp.logical_not(upper)

            @pl.when(goes)
            def _(block=block):
                action(message(block, slot, beam, bands))

    for slot in range(beams):
        beam = (my_group * beam_dev + slot) % beams
        wide = x_ref[beam].astype(jnp.float32)
        normed = ((wide - channel_mean) * channel_scale).astype(jnp.bfloat16)
        sums = jnp.dot(chosen, normed, preferred_element_type=jnp.float32)
        tree = [[sums[i * bands:(i + 1) * bands]] for i in range(blocks)]
        while len(tree) > 1:
            merged = []
            for low, high in zip(tree[0::2], tree[1::2]):
                merged.append(
                    [low[m // 2] + earlier(high[m // 2], (m + 1) // 2) for m in range(2 * len(low))]
                )
            tree = merged
        for number, row in enumerate(tree[0]):
            if fold:
                both = row[:half] + row[half:]
                row = jnp.concatenate([jnp.where(upper, both, row[:half]), row[half:]], axis=0)
            send[number, slot] = row.astype(jnp.bfloat16)
        if slot == 0:
            pl.semaphore_wait(barrier, devices - 1)
        every_message(lambda copy: copy.start(), slot)
        if slot < beam_dev:
            own_copy(slot, slot).start()

    for slot in range(beam_dev):
        own_copy(slot, slot).wait()
    limit = sum(jnp.where(my_block == block, limits[block], 0) for block in range(blocks))
    for place in range(devices):
        for part in range(beam_dev):
            rows = bands // 2 if fold and 2 * place >= devices else bands
            target = out_ref.at[part, place, pl.ds(0, rows)]
            @pl.when((place * width < limit) & (place != my_place))
            def _(target=target, place=place, part=part):
                pltpu.make_async_remote_copy(
                    src_ref=target, dst_ref=target, send_sem=send_sem.at[0, 0],
                    recv_sem=recv_sem.at[part, place],
                    device_id={"freq": my_block, "beam": my_group},
                    device_id_type=pl.DeviceIdType.MESH,
                ).wait_recv()
    for slot in range(beams):
        every_message(lambda copy: copy.wait_send(), slot)


def entry_rows(intensity, channel_mask):
    beams, width, samples = intensity.shape
    blocks, groups = lax.axis_size("freq"), lax.axis_size("beam")
    bands = width * NDM // (CHANS * blocks)
    beam_dev, devices = beams // groups, blocks * groups
    return pl.pallas_call(
        entry_kernel,
        in_specs=[pl.BlockSpec(memory_space=pl.ANY), pl.BlockSpec(memory_space=pltpu.VMEM)],
        out_specs=pl.BlockSpec(memory_space=pl.ANY),
        scratch_shapes=[
            pltpu.VMEM((beams, width, samples), jnp.bfloat16),
            pltpu.SemaphoreType.DMA((4,)),
            pltpu.VMEM((blocks, beams, bands, samples), jnp.bfloat16),
            pltpu.SemaphoreType.DMA((blocks, beams)),
            pltpu.SemaphoreType.DMA((beam_dev, devices)),
            pltpu.SemaphoreType.DMA((beam_dev,)),
        ],
        out_shape=jax.ShapeDtypeStruct((beam_dev, devices, bands, samples), jnp.bfloat16),
        compiler_params=pltpu.CompilerParams(collective_id=0, has_side_effects=True),
    )(intensity, channel_mask.reshape(1, -1))


def advanced(pieces, amount):
    lanes = pieces[0].shape[-1]
    position = lane_index(pieces[0].shape)
    turn = (lanes - amount) & (lanes - 1)
    turned = [pltpu.roll(piece, turn, 1) for piece in pieces]
    return joined(turned, lambda limit: position < limit - amount)


def advanced_rows(pieces, amounts):
    lanes = pieces[0].shape[-1]
    position = lane_index(pieces[0].shape) + amounts
    picks = position & (lanes - 1)
    turned = [jnp.take_along_axis(piece, picks, axis=1, mode="promise_in_bounds") for piece in pieces]
    return joined(turned, lambda limit: position < limit)


def joined(turned, below):
    lanes = turned[0].shape[-1]
    near = [below((k + 1) * lanes) for k in range(len(turned))]
    result = []
    for number in range(len(turned)):
        value = jnp.zeros_like(turned[0])
        for ahead in reversed(range(len(turned) - number)):
            value = jnp.where(near[ahead], turned[number + ahead], value)
        result.append(value)
    return result


def trial_kernel(place_ref, widths_ref, x_ref, out_ref, first, even, odd, series, prefix):
    total, samples = out_ref.shape[2], x_ref.shape[3]
    tiles = total // LANE_ROWS
    tile_bits = tiles.bit_length() - 1
    lanes = prefix.shape[2]
    parts = samples // lanes
    pitch = first.shape[1] // LANE_ROWS
    block = place_ref[0]
    bands = x_ref.shape[2]
    fold = folds(total, samples)
    half_bands = bands // 2
    sources = x_ref.shape[1]
    for number in range(sources):
        high, start = divmod(number * bands, tiles)
        start += reverse_bits(high, LANE_ROWS.bit_length() - 1) * pitch
        for part in range(parts):
            cut = slice(part * lanes, (part + 1) * lanes)
            if fold and 2 * number >= sources:
                first[part, start:start + half_bands] = x_ref[0, number, :half_bands, cut].astype(jnp.float32)
                first[part, start + half_bands:start + bands] = jnp.zeros((half_bands, lanes), jnp.float32)
            else:
                first[part, start:start + bands] = x_ref[0, number, :, cut].astype(jnp.float32)
    for tile in range(tiles):
        spot = tile
        if fold:
            band = tile % bands
            spot = tile - band + (band % 2) * half_bands + band // 2
        for part in range(parts):
            even[reverse_bits(tile, tile_bits), :, part * lanes:(part + 1) * lanes] = first[
                part, pl.ds(spot, LANE_ROWS, stride=pitch)
            ]

    source, target = even, odd
    count = 1
    while count < tiles:
        half = tiles // count // 2

        def merge(j, source=source, target=target, count=count, half=half):
            flat = (half * LANE_ROWS, lanes)
            cut = [slice(part * lanes, (part + 1) * lanes) for part in range(parts)]
            low = [source[pl.ds(j * 2 * half, half), :, c].reshape(flat) for c in cut]
            high = [source[pl.ds(j * 2 * half + half, half), :, c].reshape(flat) for c in cut]
            for side in range(2):
                moved = advanced(high, block * count + j + side)
                for c, base, extra in zip(cut, low, moved):
                    target[pl.ds((2 * j + side) * half, half), :, c] = (base + extra).reshape(
                        half, LANE_ROWS, lanes
                    )

        if count <= 16:
            for j in range(count):
                merge(j)
        else:
            def step(i, carry, merge=merge):
                for k in range(32):
                    merge(i * 32 + k)
                return carry
            lax.fori_loop(0, count // 32, step, 0)
        source, target = target, source
        count = count * 2

    spot = lax.broadcasted_iota(jnp.int32, (LANE_ROWS, lanes), 0)
    bits = [spot >> 2 & 1, spot >> 1 & 1, spot & 1]
    clear = [bit == 0 for bit in bits]

    def final_rows(j):
        pieces = [source[j, :, part * lanes:(part + 1) * lanes] for part in range(parts)]
        row = spot * 0 + (block * tiles + j)
        for level, reach in enumerate((4, 2, 1)):
            low, high = [], []
            for piece in pieces:
                down = pltpu.roll(piece, reach, 0)
                up = down if 2 * reach == LANE_ROWS else pltpu.roll(piece, LANE_ROWS - reach, 0)
                low.append(jnp.where(clear[level], piece, down))
                high.append(jnp.where(clear[level], up, piece))
            moved = advanced_rows(high, row + bits[level])
            pieces = [base + extra for base, extra in zip(low, moved)]
            row = 2 * row + bits[level]
        return jnp.concatenate(pieces, axis=1)

    def finish(i, carry):
        for k in range(16):
            pair = i * 16 + k
            rows = jnp.concatenate([final_rows(2 * pair), final_rows(2 * pair + 1)], axis=0)
            coarse = rows.astype(jnp.bfloat16)
            place = pl.ds(pl.multiple_of(pair * 16, 16), 16)
            series[place, :samples] = coarse
            series[place, samples:] = (rows - coarse.astype(jnp.float32)).astype(jnp.bfloat16)
        return carry

    lax.fori_loop(0, tiles // 32, finish, 0)

    until = lax.broadcasted_iota(jnp.int32, (samples, 2 * samples), 0)
    time = lax.broadcasted_iota(jnp.int32, (samples, 2 * samples), 1) & (samples - 1)
    ladder = jnp.where(time <= until, 1.0, 0.0).astype(jnp.bfloat16)
    margin = prefix.shape[1] - samples - LANE_ROWS
    piece = 2 * lanes
    for part in range(total // piece):
        sums = lax.dot_general(
            ladder, series[part * piece:(part + 1) * piece], (((1,), (1,)), ((), ())),
            preferred_element_type=jnp.float32,
        )
        for side in range(2):
            column = 2 * part + side
            prefix[column, :LANE_ROWS] = jnp.zeros((LANE_ROWS, lanes), jnp.float32)
            prefix[column, LANE_ROWS:LANE_ROWS + samples] = sums[:, side * lanes:(side + 1) * lanes]
            prefix[column, LANE_ROWS + samples:] = jnp.full((margin, lanes), -jnp.inf, jnp.float32)
    for column in range(total // lanes):
        best = None
        for number in range(widths_ref.shape[0]):
            width = widths_ref[number]
            sums = (
                prefix[column, pl.ds(LANE_ROWS - 1 + width, samples)]
                - prefix[column, LANE_ROWS - 1:LANE_ROWS - 1 + samples]
            )
            norm = lax.rsqrt(jnp.full((1, lanes), width * CHANS, jnp.int32).astype(jnp.float32))
            peak = jnp.max(sums, axis=0, keepdims=True) * norm
            best = peak if best is None else jnp.maximum(best, peak)
        out_ref[0, :, column * lanes:(column + 1) * lanes] = best


def trial_peaks(rows, box_widths, place):
    beams, devices, bands, samples = rows.shape
    total = devices * bands
    tiles = total // LANE_ROWS
    return pl.pallas_call(
        trial_kernel,
        grid_spec=pltpu.PrefetchScalarGridSpec(
            num_scalar_prefetch=2,
            grid=(beams,),
            in_specs=[pl.BlockSpec((1, devices, bands, samples), lambda b, p, w: (b, 0, 0, 0))],
            out_specs=pl.BlockSpec((1, 1, total), lambda b, p, w: (b, 0, 0)),
            scratch_shapes=[
                pltpu.VMEM((samples // LANES, total + LANE_ROWS * LANE_ROWS, LANES), jnp.float32),
                pltpu.VMEM((tiles, LANE_ROWS, samples), jnp.float32),
                pltpu.VMEM((tiles, LANE_ROWS, samples), jnp.float32),
                pltpu.VMEM((total, 2 * samples), jnp.bfloat16),
                pltpu.VMEM((total // LANES, LANE_ROWS + samples + WIDEST, LANES), jnp.float32),
            ],
        ),
        out_shape=jax.ShapeDtypeStruct((beams, 1, total), jnp.float32),
    )(place, box_widths, rows)[:, 0]


def shards(intensity, channel_mask, box_widths):
    rows = entry_rows(intensity, channel_mask)
    return trial_peaks(rows, box_widths, lax.axis_index("freq").reshape(1))


def solution(mesh):
    in_specs = (P(None, ("freq", "beam"), None), P("freq"), P())
    out_specs = P("beam", "freq")
    return jax.shard_map(shards, mesh=mesh, in_specs=in_specs, out_specs=out_specs, check_vma=False)
```
